32 devices in a mesh: fsdp: 4 (over x, core), ctx: 8 (over z, y).
Axes of the slice: x: 2, y: 2, z: 4, core: 2. Of those that a mesh axis runs over, the one named last changes fastest.
Arguments:
- hidden_in: float32 [4096, 2048], P(('fsdp', 'ctx')), may hold values from -6 to 6
- doc_start: int32 [4096], P(('fsdp', 'ctx')), may hold values 0 or 1
- routes: int32 [4096, 8], P(('fsdp', 'ctx')), may hold values from 0 to 15, all different within a row; in each aligned block of 128 rows (0 to 127, 128 to 255, ...) at most 91 rows name the same one
- gate_weights: float32 [4096, 8], P(('fsdp', 'ctx')), may hold values from 0.1 to 1
- w_query: bfloat16 [2048, 2048], P(('fsdp', 'ctx')), may hold values from -0.125 to 0.125
- w_key: bfloat16 [2048, 2048], P(('fsdp', 'ctx')), may hold values from -0.125 to 0.125
- w_value: bfloat16 [2048, 2048], P(('fsdp', 'ctx')), may hold values from -0.125 to 0.125
- w_output: bfloat16 [2048, 2048], P(('fsdp', 'ctx')), may hold values from -3 to 3
- gain_attention: bfloat16 [2048], P(('fsdp', 'ctx')), may hold values from 0.5 to 1.5
- gain_experts: bfloat16 [2048], P(('fsdp', 'ctx')), may hold values from 0.5 to 1.5
- gain_query: bfloat16 [2048], P(('fsdp', 'ctx')), may hold values from 0.5 to 1.5
- gain_key: bfloat16 [2048], P(('fsdp', 'ctx')), may hold values from 0.5 to 1.5
- expert_gate: bfloat16 [16, 2048, 1024], P('ctx', 'fsdp'), may hold values from -0.125 to 0.125
- expert_up: bfloat16 [16, 2048, 1024], P('ctx', 'fsdp'), may hold values from -0.125 to 0.125
- expert_down: bfloat16 [16, 1024, 2048], P('ctx', None, 'fsdp'), may hold values from -0.1875 to 0.1875
- cotangent: float32 [4096, 2048], P(('fsdp', 'ctx')), may hold values from -6 to 6
Outputs:
- hidden_out: float32 [4096, 2048], P(('fsdp', 'ctx'))
- grad_hidden: float32 [4096, 2048], P(('fsdp', 'ctx'))
- grad_w_query: float32 [2048, 2048], P(('fsdp', 'ctx'))
- grad_w_key: float32 [2048, 2048], P(('fsdp', 'ctx'))
- grad_w_value: float32 [2048, 2048], P(('fsdp', 'ctx'))
- grad_w_output: float32 [2048, 2048], P(('fsdp', 'ctx'))
- grad_gain_attention: float32 [2048], P(('fsdp', 'ctx'))
- grad_gain_experts: float32 [2048], P(('fsdp', 'ctx'))
- grad_gain_query: float32 [2048], P(('fsdp', 'ctx'))
- grad_gain_key: float32 [2048], P(('fsdp', 'ctx'))
- grad_expert_gate: float32 [16, 2048, 1024], P('ctx', 'fsdp')
- grad_expert_up: float32 [16, 2048, 1024], P('ctx', 'fsdp')
- grad_expert_down: float32 [16, 1024, 2048], P('ctx', None, 'fsdp')
The draws below stay inside these ranges and needn't reach their ends.
Inputs may be any that keep to these rules, and one draw needn't show every extreme that they name: `routes`: within the rows of one device, each expert is named by at most 91 rows.
All inputs are finite; a program needn't handle non-finite values. No bound on the sum of `doc_start` on one device may be relied on, other than what follows from the above.
Results may differ from the reference program's by a relative error of at most 0.029.
Values may be sent and summed in bfloat16 or wider, within the bound.
No kernel may reach another device: no remote copies, remote signals or barrier semaphores. Data moves between devices by JAX's collectives and lax.ppermute only.
A program may use at most 384 MiB of HBM per device.

```python
import math
import jax
import jax.numpy as jnp
import numpy as np
from jax import lax

D = 2048
HEADS = 16
HD = 128
FF = 1024
TOPK = 8
TOK_DEV = 128
EXPERTS = 16
STREAM = 1024
TOKENS = 4096
CAP = 91
N_FSDP = 4


def plant(array, rng, least, top_value):
    longest = array.shape.index(max(array.shape))
    spots = []
    for shift in (0, 1):
        where = [jax.random.randint(jax.random.fold_in(rng, axis), (), 0, length) for axis, length in enumerate(array.shape)]
        where[longest] = (where[longest] + shift) % array.shape[longest]
        spots.append(tuple(where))
    return array.at[spots[0]].set(least).at[spots[1]].set(top_value)


def spiked(entries, own_key, source, target, blocks, factor):
    def block_of(dim):
        return (jnp.arange(entries.shape[dim]) // (entries.shape[dim] // blocks)).reshape((-1,) + (1,) * (entries.ndim - 1 - dim))

    near = jax.random.permutation(own_key, blocks)[block_of(target)]
    far = (block_of(target) + blocks // 2) % blocks
    return jnp.where((block_of(source) == near) | (block_of(source) == far), factor * entries, entries)


def block_scale(stream_key, extent, split, smallest, high):
    gain = 1.0
    for dim, shards_of in split:
        heights = jax.random.uniform(jax.random.fold_in(jax.random.fold_in(stream_key, 6), dim), (shards_of,), jnp.float32, smallest / len(split), high / len(split))
        gain = gain * jnp.repeat(jnp.exp(heights), extent[dim] // shards_of).reshape((-1,) + (1,) * (len(extent) - 1 - dim))
    return gain


def deal_out(rng, own, number, rows, number_of, top, limit, lean):
    sequence = jax.random.permutation(rng, number_of)
    crowded, common = load_shares(number_of, rows * top, limit, lean, True), load_shares(number_of, rows * top, limit, lean, False)
    places = jnp.arange(number_of)

    def named(sizes, rotation):
        used = int((sizes > 0).sum())
        fixed = max(1, used // 4)
        moved = fixed + (places - fixed + rotation * (used - fixed)) % max(1, number_of - fixed)
        return jnp.zeros((number_of,), jnp.int32).at[sequence[jnp.where(places < fixed, places, moved)]].set(jnp.asarray(sizes, jnp.int32))

    sizes = jnp.where(number % 4 == 0, named(crowded, number // 4), named(common, number - number // 4 - 1))
    mixed = jax.random.permutation(jax.random.fold_in(own, 3), number_of)
    donor, receiver = mixed[0:number_of // 2 * 2:2], mixed[1:number_of // 2 * 2:2]
    margin = jnp.minimum(sizes[donor] - 1, limit - sizes[receiver]) // 2
    margin = jnp.where((donor == sequence[0]) | (receiver == sequence[0]) | (sizes[receiver] == 0), 0, jnp.maximum(margin, 0))
    moved = jax.random.randint(jax.random.fold_in(own, 4), (number_of // 2,), 0, 1 << 20) % (margin + 1)
    sizes = sizes.at[donor].add(-moved).at[receiver].add(moved)
    labels = jnp.searchsorted(jnp.cumsum(sizes), jnp.arange(rows * top), side="right").astype(jnp.int32)
    listing = labels.reshape(top, rows).T
    listing = listing[jax.random.permutation(jax.random.fold_in(own, 1), rows)]
    rotation = jax.random.randint(jax.random.fold_in(own, 2), (rows, 1), 0, top)
    return jnp.take_along_axis(listing, (jnp.arange(top)[None, :] + rotation) % top, axis=1)


def load_shares(number_of, total, limit, skew, full):
    weights = [(1 << 20) // math.isqrt(grade ** skew) + 1 for grade in range(1, number_of + 1)]
    largest = limit if full else min(limit, max(-(-total // number_of), total * weights[0] // sum(weights)))
    least = 1 if total - largest >= number_of - 1 else 0
    given, surplus = [largest] + [least] * (number_of - 1), total - largest - least * (number_of - 1)
    while surplus > 0:
        movable = [i for i in range(1, number_of) if given[i] < largest] or [i for i in range(1, number_of) if given[i] < limit]
        mass, budget = sum([weights[i] for i in movable]), surplus
        for i in movable:
            addition = min(limit - given[i], max(1, budget * weights[i] // mass), surplus)
            given[i] = given[i] + addition
            surplus = surplus - addition
    return np.array(given)


def noise(key, extent, width, bound, split=(), kind=jnp.bfloat16):
    result = width * jax.random.normal(key, extent, jnp.float32)
    if split:
        result = result * block_scale(key, extent, split, -0.22, 0.18)
    return jnp.clip(result, -bound, bound).astype(kind)


def bell_draw_with(key, shape, width, reach, cuts, heavy, kind=jnp.bfloat16):
    result = width * jax.random.normal(key, shape, jnp.float32)
    if cuts:
        result = result * block_scale(key, shape, cuts, -0.22, 0.18)
    return jnp.clip(spiked(result, jax.random.fold_in(key, 3), *heavy), -reach, reach).astype(kind)


def setup_inputs(seed: int = 0) -> dict:
    key_of = jax.random.split(jax.random.key(seed), 17)
    hidden_in = noise(key_of[0], (TOKENS, D), 1.0, 6.0, ((0, 32),), jnp.float32)
    doc_start = plant((jax.random.randint(key_of[1], (TOKENS,), 0, 4 * TOK_DEV) < 1).astype(jnp.int32), jax.random.fold_in(key_of[1], 1), 0, 1)
    routes_keys = jax.random.split(jax.random.fold_in(key_of[2], 1), TOKENS // TOK_DEV)
    routes_turns = jax.random.permutation(jax.random.fold_in(key_of[2], 3), TOKENS // TOK_DEV)
    routes = jax.vmap(lambda own, number: deal_out(jax.random.fold_in(key_of[2], 2), own, number, TOK_DEV, EXPERTS, TOPK, CAP, 0))(routes_keys, routes_turns).reshape((TOKENS, TOPK))
    gate_weights = jnp.clip(jnp.exp(math.log(1.0) - 2.3025851 * jax.random.uniform(key_of[3], (TOKENS, TOPK), jnp.float32) ** block_scale(key_of[3], (TOKENS, TOPK), ((0, 32),), -0.2, 0.2)), 0.1, 1.0)
    w_query = noise(key_of[4], (D, D), D ** -0.5, 0.125, ((0, 32),))
    w_key = noise(key_of[5], (D, D), D ** -0.5, 0.125, ((0, 32),))
    w_value = noise(key_of[6], (D, D), D ** -0.5, 0.125, ((0, 32),))
    w_output = noise(key_of[7], (D, D), (max(1, D // (4 * TOK_DEV))) ** -0.5, 3.0, ((0, 32),))
    gain_attention = jnp.clip(1.0 + 0.1 * jax.random.normal(key_of[8], (D,), jnp.float32), 0.5, 1.5).astype(jnp.bfloat16)
    gain_experts = jnp.clip(1.0 + 0.1 * jax.random.normal(key_of[9], (D,), jnp.float32), 0.5, 1.5).astype(jnp.bfloat16)
    gain_query = jnp.clip(1.0 + 0.1 * jax.random.normal(key_of[10], (D,), jnp.float32), 0.5, 1.5).astype(jnp.bfloat16)
    gain_key = jnp.clip(1.0 + 0.1 * jax.random.normal(key_of[11], (D,), jnp.float32), 0.5, 1.5).astype(jnp.bfloat16)
    expert_gate = noise(key_of[12], (EXPERTS, D, FF), D ** -0.5, 0.125, ((0, 8), (1, 4)))
    expert_up = noise(key_of[13], (EXPERTS, D, FF), D ** -0.5, 0.125, ((0, 8), (1, 4)))
    expert_down = noise(key_of[14], (EXPERTS, FF, D), FF ** -0.5, 0.1875, ((0, 8), (2, 4)))
    cotangent = bell_draw_with(key_of[15], (TOKENS, D), 1.0, 6.0, ((0, 32),), (0, 1, 32, 2.75), jnp.float32)
    return dict(hidden_in=hidden_in, doc_start=doc_start, routes=routes, gate_weights=gate_weights, w_query=w_query, w_key=w_key, w_value=w_value, w_output=w_output, gain_attention=gain_attention, gain_experts=gain_experts, gain_query=gain_query, gain_key=gain_key, expert_gate=expert_gate, expert_up=expert_up, expert_down=expert_down, cotangent=cotangent)


epsilon = 1e-06
rope_base = 10000.0
masked_score = -1e+30

@jax.custom_vjp
def low(v):
    return lax.optimization_barrier(v.astype(jnp.bfloat16)).astype(jnp.float32)

@jax.custom_vjp
def low_back(v):
    return v

def low_keep(v):
    return (low(v), None)

def low_pass(kept, grad):
    return (grad,)

def back_keep(v):
    return (v, None)

def back_low(kept, grad):
    return (low(grad),)
low.defvjp(low_keep, low_pass)
low_back.defvjp(back_keep, back_low)

def highest(einsum_form, left_side, right_side):
    return jnp.einsum(einsum_form, left_side, right_side, precision=lax.Precision.HIGHEST, preferred_element_type=jnp.float32)

def rms_scale(values):
    return lax.rsqrt(lax.optimization_barrier(jnp.mean(values * values, axis=-1, keepdims=True)) + epsilon)

def rotate(values, cosine, sine_table):
    half_width = values.shape[-1] // 2
    leading = values[..., :half_width]
    trailing = values[..., half_width:]
    return jnp.concatenate([leading * cosine - trailing * sine_table, trailing * cosine + leading * sine_table], axis=-1)

def one_stream(params, element):
    w_query, w_key, w_value, w_output, gain_attention, gain_experts, gain_query, gain_key, expert_gate, expert_up, expert_down = params
    hidden, starts, routes, gate_weights = element
    length = hidden.shape[0]
    where_idx = jnp.arange(length, dtype=jnp.int32)
    segment = jnp.cumsum(starts)
    last_start = lax.cummax(jnp.where(starts == 1, where_idx, 0), axis=0)
    position = (where_idx - last_start).astype(jnp.float32)
    normed = low(hidden * rms_scale(hidden) * gain_attention)
    queries = low_back(highest('td,de->te', normed, w_query))
    keys_pre = low_back(highest('td,de->te', normed, w_key))
    values_pre = low_back(highest('td,de->te', normed, w_value))
    queries = queries * rms_scale(queries) * gain_query
    keys_pre = keys_pre * rms_scale(keys_pre) * gain_key
    frequency = rope_base ** (-jnp.arange(HD // 2, dtype=jnp.float32) * 2.0 / HD)
    angles = position[:, None] * frequency[None, :]
    cosine = jnp.cos(angles)[:, None, :]
    sine_table = jnp.sin(angles)[:, None, :]
    query_rot = low(rotate(queries.reshape(length, HEADS, HD), cosine, sine_table) * HD ** (-0.5))
    key_rot = low(rotate(keys_pre.reshape(length, HEADS, HD), cosine, sine_table))
    value_low = low(values_pre).reshape(length, HEADS, HD)
    block_rows = 512 if length % 512 == 0 else length

    def attend(query_block, segment_block):
        scores = low_back(highest('qhd,khd->hqk', query_block, key_rot))
        allowed = (segment_block[:, None] == segment[None, :])[None]
        scores = jnp.where(allowed, scores, masked_score)
        weights = jnp.exp(scores - lax.optimization_barrier(jnp.max(scores, axis=-1, keepdims=True)))
        weights = weights / lax.optimization_barrier(jnp.sum(weights, axis=-1, keepdims=True))
        return highest('hqk,khd->qhd', low(weights), value_low)

    def attend_block(pieces):
        return jax.checkpoint(attend)(pieces[0], pieces[1])
    attended = lax.map(attend_block, (query_rot.reshape(length // block_rows, block_rows, HEADS, HD), segment.reshape(length // block_rows, block_rows)))
    attended = low(low_back(attended.reshape(length, D)))
    mixed = hidden + low_back(highest('td,de->te', attended, w_output))
    normed_two = low(mixed * rms_scale(mixed) * gain_experts)
    blocks_total = length // TOK_DEV
    flat_routes = routes.reshape(blocks_total, TOK_DEV * TOPK)
    onehot = (flat_routes[:, :, None] == jnp.arange(EXPERTS, dtype=jnp.int32)[None, None, :]).astype(jnp.int32)
    slot_index = lax.optimization_barrier(jnp.sum((jnp.cumsum(onehot, axis=1) - 1) * onehot, axis=-1))
    block_id = jnp.arange(blocks_total, dtype=jnp.int32)[:, None]
    target = (flat_routes * (blocks_total * CAP) + block_id * CAP + slot_index).reshape(-1)
    slot_total = EXPERTS * blocks_total * CAP
    assignment = jnp.zeros((slot_total,), jnp.int32).at[target].set(jnp.arange(length * TOPK, dtype=jnp.int32))
    filled = jnp.zeros((slot_total,), jnp.int32).at[target].set(1)
    copies = low_back(jnp.broadcast_to(normed_two[:, None, :], (length, TOPK, D))).reshape(length * TOPK, D)
    expert_rows = jnp.where(filled[:, None] == 1, copies[assignment], 0.0).reshape(EXPERTS, blocks_total * CAP, D)
    gate_pre = low_back(highest('end,edf->enf', expert_rows, expert_gate))
    up_pre = low_back(highest('end,edf->enf', expert_rows, expert_up))
    activated = low(jax.nn.silu(gate_pre) * up_pre)
    produced = low(low_back(highest('enf,efd->end', activated, expert_down))).reshape(slot_total, D)
    picked = produced[target].reshape(length, TOPK, D)
    return mixed + highest('tk,tkd->td', gate_weights, picked)

def reference(hidden_in, doc_start, routes, gate_weights, w_query, w_key, w_value, w_output, gain_attention, gain_experts, gain_query, gain_key, expert_gate, expert_up, expert_down, cotangent):
    params = tuple((matrix.astype(jnp.float32) for matrix in (w_query, w_key, w_value, w_output, gain_attention, gain_experts, gain_query, gain_key, expert_gate, expert_up, expert_down)))
    hidden = hidden_in.astype(jnp.float32)
    streams = N_FSDP

    def forward(params, hidden):

        def per_stream(element):
            return one_stream(params, element)
        return lax.map(per_stream, (hidden.reshape(streams, STREAM, D), doc_start.reshape(streams, STREAM), routes.reshape(streams, STREAM, TOPK), gate_weights.reshape(streams, STREAM, TOPK).astype(jnp.float32))).reshape(TOKENS, D)
    output, pullback = jax.vjp(forward, params, hidden)
    gradients, grad_hidden = pullback(cotangent.astype(jnp.float32))
    return (output, grad_hidden, gradients[0], gradients[1], gradients[2], gradients[3], gradients[4], gradients[5], gradients[6], gradients[7], gradients[8], gradients[9], gradients[10])
```

```python
import jax
import jax.numpy as jnp
import numpy as np
from jax import lax
from jax.sharding import PartitionSpec as P


HEADS = 16
HD = 128
TOPK = 8


epsilon = 1e-06
rope_base = 10000.0
masked_score = -1e30


def rms_scale(values):
    return lax.rsqrt(jnp.mean(values * values, axis=-1, keepdims=True) + epsilon)


def rotate(values, cosine, sine_table):
    half_width = values.shape[-1] // 2
    leading = values[..., :half_width]
    trailing = values[..., half_width:]
    return jnp.concatenate(
        [leading * cosine - trailing * sine_table, trailing * cosine + leading * sine_table],
        axis=-1,
    )


def rotate_back(values, cosine, sine_table):
    half_width = values.shape[-1] // 2
    leading = values[..., :half_width]
    trailing = values[..., half_width:]
    return jnp.concatenate(
        [leading * cosine + trailing * sine_table, trailing * cosine - leading * sine_table],
        axis=-1,
    )


def norm_back(grad_out, pre_norm, scale_rows, gain_full):
    scaled = pre_norm * scale_rows
    weighted = grad_out * gain_full
    grad_pre = scale_rows * (
        weighted - scaled * jnp.mean(scaled * weighted, axis=-1, keepdims=True)
    )
    return (grad_pre, jnp.sum(grad_out * scaled, axis=0))


def times_transpose(left_side, right_side):
    return lax.dot_general(
        left_side, right_side, (((1,), (1,)), ((), ())), preferred_element_type=jnp.float32
    )


def key_block_size():
    return 512


def attention_weights(
    w_query, w_key, w_value, w_output, gain_attention, gain_experts, gain_query, gain_key
):
    return (
        lax.all_gather(w_query, ("fsdp", "ctx"), axis=0, tiled=True),
        lax.all_gather(w_key, ("fsdp", "ctx"), axis=0, tiled=True),
        lax.all_gather(w_value, ("fsdp", "ctx"), axis=0, tiled=True),
        lax.all_gather(w_output, ("fsdp", "ctx"), axis=0, tiled=True),
        lax.all_gather(gain_attention, ("fsdp", "ctx"), axis=0, tiled=True),
        lax.all_gather(gain_experts, ("fsdp", "ctx"), axis=0, tiled=True),
        lax.all_gather(gain_query, ("fsdp", "ctx"), axis=0, tiled=True),
        lax.all_gather(gain_key, ("fsdp", "ctx"), axis=0, tiled=True),
    )


def per_device(
    hidden_in,
    doc_start,
    routes,
    gate_weights,
    w_query,
    w_key,
    w_value,
    w_output,
    gain_attention,
    gain_experts,
    gain_query,
    gain_key,
    expert_gate,
    expert_up,
    expert_down,
    cotangent,
):
    tok_rows = hidden_in.shape[0]
    model_width = hidden_in.shape[1]
    ctx_size = lax.axis_size("ctx")
    start_flags = lax.all_gather(doc_start, "ctx", axis=0, tiled=True)
    stream_len = start_flags.shape[0]
    positions_all = jnp.arange(stream_len, dtype=jnp.int32)
    segment_all = jnp.cumsum(start_flags)
    last_start = lax.cummax(jnp.where(start_flags == 1, positions_all, 0), axis=0)
    offset = lax.axis_index("ctx") * tok_rows
    my_segment = lax.dynamic_slice_in_dim(segment_all, offset, tok_rows)
    my_position = lax.dynamic_slice_in_dim(positions_all - last_start, offset, tok_rows).astype(
        jnp.float32
    )
    segment_low = my_segment[0]
    segment_high = my_segment[tok_rows - 1]
    gathered = attention_weights(
        w_query, w_key, w_value, w_output, gain_attention, gain_experts, gain_query, gain_key
    )
    (
        query_matrix,
        key_matrix,
        value_matrix,
        output_matrix,
        attention_gain,
        expert_gain,
        query_gain,
        key_gain,
    ) = gathered
    attention_gain = attention_gain.astype(jnp.float32)
    expert_gain = expert_gain.astype(jnp.float32)
    query_gain = query_gain.astype(jnp.float32)
    key_gain = key_gain.astype(jnp.float32)
    scale_one = rms_scale(hidden_in)
    normed = (hidden_in * scale_one * attention_gain).astype(jnp.bfloat16)
    queries_pre = jnp.dot(normed, query_matrix, preferred_element_type=jnp.float32)
    keys_pre = jnp.dot(normed, key_matrix, preferred_element_type=jnp.float32)
    values_pre = jnp.dot(normed, value_matrix, preferred_element_type=jnp.float32)
    query_scale = rms_scale(queries_pre)
    key_scale = rms_scale(keys_pre)
    frequency = rope_base ** (-jnp.arange(HD // 2, dtype=jnp.float32) * 2.0 / HD)
    angles = my_position[:, None] * frequency[None, :]
    cosine = jnp.cos(angles)[:, None, :]
    sine_table = jnp.sin(angles)[:, None, :]
    query_rot = (
        rotate(
            (queries_pre * query_scale * query_gain).reshape(tok_rows, HEADS, HD),
            cosine,
            sine_table,
        )
        * HD ** (-0.5)
    ).astype(jnp.bfloat16)
    key_rot = rotate(
        (keys_pre * key_scale * key_gain).reshape(tok_rows, HEADS, HD), cosine, sine_table
    ).astype(jnp.bfloat16)
    value_low = values_pre.astype(jnp.bfloat16).reshape(tok_rows, HEADS, HD)
    initial = (
        jnp.zeros((HEADS, tok_rows, HD), jnp.float32),
        jnp.full((HEADS, tok_rows), masked_score, jnp.float32),
        jnp.zeros((HEADS, tok_rows), jnp.float32),
    )
    piece_keys = lax.all_gather(key_rot, "ctx", axis=0, tiled=True)
    piece_values = lax.all_gather(value_low, "ctx", axis=0, tiled=True)
    count_rows = piece_keys.shape[0]
    touching = (segment_all[0] <= segment_high) & (segment_low <= segment_all[count_rows - 1])

    def forward_compute(state_in):
        block_size = key_block_size()

        def forward_advance(state_now, block_in):
            block_keys, block_values, block_segment = block_in
            accumulated, running_max, running_sum = state_now
            scores = jnp.einsum(
                "qhd,khd->hqk", query_rot, block_keys, preferred_element_type=jnp.float32
            )
            allowed = (my_segment[:, None] == block_segment[None, :])[None]
            block_max = jnp.max(jnp.where(allowed, scores, masked_score), axis=-1)
            new_max = jnp.maximum(running_max, block_max)
            factor = jnp.exp(running_max - new_max)
            softmax_part = jnp.where(allowed, jnp.exp(scores - new_max[..., None]), 0.0)
            running_sum = running_sum * factor + jnp.sum(softmax_part, axis=-1)
            accumulated = accumulated * factor[..., None] + jnp.einsum(
                "hqk,khd->hqd",
                softmax_part.astype(jnp.bfloat16),
                block_values,
                preferred_element_type=jnp.float32,
            )
            return ((accumulated, new_max, running_sum), None)

        blocks_in = (
            piece_keys.reshape(count_rows // block_size, block_size, HEADS, HD),
            piece_values.reshape(count_rows // block_size, block_size, HEADS, HD),
            segment_all.reshape(count_rows // block_size, block_size),
        )
        return lax.scan(forward_advance, state_in, blocks_in)[0]

    def forward_unchanged(state_in):
        return state_in

    accumulated, running_max, running_sum = lax.cond(
        touching, forward_compute, forward_unchanged, initial
    )
    attended_heads = jnp.transpose(accumulated / running_sum[..., None], (1, 0, 2))
    lse_local = running_max + jnp.log(running_sum)
    attended_low = attended_heads.reshape(tok_rows, model_width).astype(jnp.bfloat16)
    mixed = hidden_in + jnp.dot(attended_low, output_matrix, preferred_element_type=jnp.float32)
    scale_two = rms_scale(mixed)
    normed_two = (mixed * scale_two * expert_gain).astype(jnp.bfloat16)
    gate_full, up_full, down_full = (
        lax.all_gather(expert_gate, "fsdp", axis=1, tiled=True),
        lax.all_gather(expert_up, "fsdp", axis=1, tiled=True),
        lax.all_gather(expert_down, "fsdp", axis=2, tiled=True),
    )
    local_experts = expert_gate.shape[0]
    total_experts = local_experts * ctx_size
    capacity = min(tok_rows, tok_rows * TOPK * 10 // (7 * total_experts))
    flat_routes = routes.reshape(-1)
    assign_total = flat_routes.shape[0]
    onehot = (flat_routes[:, None] == jnp.arange(total_experts, dtype=jnp.int32)[None, :]).astype(
        jnp.int32
    )
    slot_index = jnp.sum((jnp.cumsum(onehot, axis=0) - 1) * onehot, axis=-1)
    target = flat_routes * capacity + slot_index
    slot_total = total_experts * capacity
    assignment = (
        jnp.zeros((slot_total,), jnp.int32)
        .at[target]
        .set(jnp.arange(assign_total, dtype=jnp.int32))
    )
    filled = jnp.zeros((slot_total,), jnp.int32).at[target].set(1)
    zero_low = jnp.zeros((), jnp.bfloat16)
    send_rows = jnp.where(filled[:, None] == 1, normed_two[assignment // TOPK], zero_low).reshape(
        ctx_size, local_experts, capacity, model_width
    )
    received = lax.all_to_all(send_rows, "ctx", split_axis=0, concat_axis=0, tiled=True)
    gate_part = jnp.einsum(
        "sjnd,jdf->sjnf", received, gate_full, preferred_element_type=jnp.float32
    )
    up_part = jnp.einsum("sjnd,jdf->sjnf", received, up_full, preferred_element_type=jnp.float32)
    activated = (jax.nn.silu(gate_part) * up_part).astype(jnp.bfloat16)
    produced = jnp.einsum(
        "sjnf,jfd->sjnd", activated, down_full, preferred_element_type=jnp.float32
    ).astype(jnp.bfloat16)
    returned = lax.all_to_all(produced, "ctx", split_axis=0, concat_axis=0, tiled=True)
    returned, received, gate_pre, up_pre = (returned, received, gate_part, up_part)
    picked = returned.reshape(slot_total, model_width)[target].reshape(tok_rows, TOPK, model_width)
    hidden_out = mixed + jnp.sum(gate_weights[:, :, None] * picked.astype(jnp.float32), axis=1)
    grad_produced = (
        (gate_weights[:, :, None] * cotangent[:, None, :])
        .astype(jnp.bfloat16)
        .reshape(assign_total, model_width)
    )
    grad_send = jnp.where(filled[:, None] == 1, grad_produced[assignment], zero_low).reshape(
        ctx_size, local_experts, capacity, model_width
    )
    grad_received = lax.all_to_all(grad_send, "ctx", split_axis=0, concat_axis=0, tiled=True)
    sigmoid_gate = jax.nn.sigmoid(gate_pre)
    silu_gate = gate_pre * sigmoid_gate
    activated = (silu_gate * up_pre).astype(jnp.bfloat16)
    grad_act = jnp.einsum(
        "sjnd,jfd->sjnf", grad_received, down_full, preferred_element_type=jnp.float32
    )
    grad_gate = (grad_act * up_pre * sigmoid_gate * (1.0 + gate_pre * (1.0 - sigmoid_gate))).astype(
        jnp.bfloat16
    )
    grad_up = (grad_act * silu_gate).astype(jnp.bfloat16)
    grad_input = jnp.einsum(
        "sjnf,jdf->sjnd", grad_gate, gate_full, preferred_element_type=jnp.float32
    )
    grad_input = (
        grad_input
        + jnp.einsum("sjnf,jdf->sjnd", grad_up, up_full, preferred_element_type=jnp.float32)
    ).astype(jnp.bfloat16)
    grad_returned = lax.all_to_all(grad_input, "ctx", split_axis=0, concat_axis=0, tiled=True)
    gate_parts = []
    up_parts = []
    down_parts = []
    for expert_slot in range(local_experts):
        part_gate = jnp.einsum(
            "snd,snf->df",
            received[:, expert_slot],
            grad_gate[:, expert_slot],
            preferred_element_type=jnp.float32,
        )
        part_up = jnp.einsum(
            "snd,snf->df",
            received[:, expert_slot],
            grad_up[:, expert_slot],
            preferred_element_type=jnp.float32,
        )
        part_down = jnp.einsum(
            "snf,snd->fd",
            activated[:, expert_slot],
            grad_received[:, expert_slot],
            preferred_element_type=jnp.float32,
        )
        reduced = (
            lax.psum_scatter(
                part_gate.astype(jnp.bfloat16), "fsdp", scatter_dimension=0, tiled=True
            ).astype(jnp.float32),
            lax.psum_scatter(
                part_up.astype(jnp.bfloat16), "fsdp", scatter_dimension=0, tiled=True
            ).astype(jnp.float32),
            lax.psum_scatter(
                part_down.astype(jnp.bfloat16), "fsdp", scatter_dimension=1, tiled=True
            ).astype(jnp.float32),
        )
        gate_parts.append(reduced[0])
        up_parts.append(reduced[1])
        down_parts.append(reduced[2])
    grad_expert_gate = jnp.stack(gate_parts)
    grad_expert_up = jnp.stack(up_parts)
    grad_expert_down = jnp.stack(down_parts)
    grad_copies = grad_returned.reshape(slot_total, model_width)[target].reshape(
        tok_rows, TOPK, model_width
    )
    grad_normed_two = jnp.sum(grad_copies.astype(jnp.float32), axis=1)
    grad_mixed, expert_gain_part = norm_back(grad_normed_two, mixed, scale_two, expert_gain)
    grad_mixed = grad_mixed + cotangent
    grad_attn = grad_mixed.astype(jnp.bfloat16)
    back_matrices = attention_weights(
        w_query, w_key, w_value, w_output, gain_attention, gain_experts, gain_query, gain_key
    )
    query_back, key_back, value_back, output_back = (
        back_matrices[0],
        back_matrices[1],
        back_matrices[2],
        back_matrices[3],
    )
    grad_heads = (
        times_transpose(grad_attn, output_back).astype(jnp.bfloat16).reshape(tok_rows, HEADS, HD)
    )
    row_dots = jnp.sum(grad_heads.astype(jnp.float32) * attended_heads, axis=-1)
    dots_local = jnp.transpose(row_dots)
    zero_heads = jnp.zeros((HEADS, tok_rows, HD), jnp.float32)
    lse_rows = jnp.transpose(lse_local)
    lse_all, dots_all = (
        lax.all_gather(lse_rows, "ctx", axis=0, tiled=True),
        lax.all_gather(row_dots, "ctx", axis=0, tiled=True),
    )
    backward_piece_keys = lax.all_gather(key_rot, "ctx", axis=0, tiled=True)
    backward_piece_values = lax.all_gather(value_low, "ctx", axis=0, tiled=True)
    piece_queries = lax.all_gather(query_rot, "ctx", axis=0, tiled=True)
    piece_grads = lax.all_gather(grad_heads, "ctx", axis=0, tiled=True)
    backward_count_rows = backward_piece_keys.shape[0]
    touching = (segment_all[0] <= segment_high) & (
        segment_low <= segment_all[backward_count_rows - 1]
    )

    def backward_compute(state_in):
        block_size = key_block_size()

        def backward_advance(state_now, block_in):
            grad_query_acc, grad_key_acc, grad_value_acc = state_now
            (
                block_keys,
                block_values,
                block_queries,
                block_grads,
                block_segment,
                block_lse,
                block_dots,
            ) = block_in
            allowed = (my_segment[:, None] == block_segment[None, :])[None]
            scores = jnp.einsum(
                "qhd,khd->hqk", query_rot, block_keys, preferred_element_type=jnp.float32
            )
            softmax_part = jnp.where(allowed, jnp.exp(scores - lse_local[..., None]), 0.0)
            grad_probs = jnp.einsum(
                "qhd,khd->hqk", grad_heads, block_values, preferred_element_type=jnp.float32
            )
            grad_scores = (softmax_part * (grad_probs - dots_local[..., None])).astype(jnp.bfloat16)
            grad_query_acc = grad_query_acc + jnp.einsum(
                "hqk,khd->hqd", grad_scores, block_keys, preferred_element_type=jnp.float32
            )
            allowed_rev = (block_segment[:, None] == my_segment[None, :])[None]
            scores_rev = jnp.einsum(
                "khd,qhd->hkq", block_queries, key_rot, preferred_element_type=jnp.float32
            )
            softmax_rev = jnp.where(
                allowed_rev, jnp.exp(scores_rev - jnp.transpose(block_lse)[..., None]), 0.0
            )
            grad_probs_rev = jnp.einsum(
                "khd,qhd->hkq", block_grads, value_low, preferred_element_type=jnp.float32
            )
            grad_scores_rev = (
                softmax_rev * (grad_probs_rev - jnp.transpose(block_dots)[..., None])
            ).astype(jnp.bfloat16)
            grad_key_acc = grad_key_acc + jnp.einsum(
                "hkq,khd->hqd", grad_scores_rev, block_queries, preferred_element_type=jnp.float32
            )
            grad_value_acc = grad_value_acc + jnp.einsum(
                "hkq,khd->hqd",
                softmax_rev.astype(jnp.bfloat16),
                block_grads,
                preferred_element_type=jnp.float32,
            )
            return ((grad_query_acc, grad_key_acc, grad_value_acc), None)

        blocks_count = backward_count_rows // block_size
        blocks_in = (
            backward_piece_keys.reshape(blocks_count, block_size, HEADS, HD),
            backward_piece_values.reshape(blocks_count, block_size, HEADS, HD),
            piece_queries.reshape(blocks_count, block_size, HEADS, HD),
            piece_grads.reshape(blocks_count, block_size, HEADS, HD),
            segment_all.reshape(blocks_count, block_size),
            lse_all.reshape(blocks_count, block_size, HEADS),
            dots_all.reshape(blocks_count, block_size, HEADS),
        )
        return lax.scan(backward_advance, state_in, blocks_in)[0]

    def backward_unchanged(state_in):
        return state_in

    grad_query_rot, grad_key_rot, grad_value = lax.cond(
        touching, backward_compute, backward_unchanged, (zero_heads, zero_heads, zero_heads)
    )
    grad_query_normed = (
        rotate_back(jnp.transpose(grad_query_rot, (1, 0, 2)), cosine, sine_table) * HD ** (-0.5)
    ).reshape(tok_rows, model_width)
    grad_key_normed = rotate_back(
        jnp.transpose(grad_key_rot, (1, 0, 2)), cosine, sine_table
    ).reshape(tok_rows, model_width)
    grad_query_pre, query_gain_part = norm_back(
        grad_query_normed, queries_pre, query_scale, query_gain
    )
    grad_key_pre, key_gain_part = norm_back(grad_key_normed, keys_pre, key_scale, key_gain)
    grad_query_low = grad_query_pre.astype(jnp.bfloat16)
    grad_key_low = grad_key_pre.astype(jnp.bfloat16)
    grad_value_low = (
        jnp.transpose(grad_value, (1, 0, 2)).reshape(tok_rows, model_width).astype(jnp.bfloat16)
    )
    grad_normed = (
        times_transpose(grad_query_low, query_back)
        + times_transpose(grad_key_low, key_back)
        + times_transpose(grad_value_low, value_back)
    )
    grad_hidden, attention_gain_part = norm_back(grad_normed, hidden_in, scale_one, attention_gain)
    grad_hidden = grad_hidden + grad_mixed
    grads_projected = jnp.concatenate([grad_query_low, grad_key_low, grad_value_low], axis=1)
    projections_part = lax.dot_general(
        normed, grads_projected, (((0,), (0,)), ((), ())), preferred_element_type=jnp.float32
    )
    output_part = lax.dot_general(
        attended_low, grad_attn, (((0,), (0,)), ((), ())), preferred_element_type=jnp.float32
    )
    weight_grads = lax.psum_scatter(
        jnp.concatenate([projections_part, output_part], axis=1),
        ("fsdp", "ctx"),
        scatter_dimension=0,
        tiled=True,
    )
    gain_grads = (
        lax.psum_scatter(attention_gain_part, ("fsdp", "ctx"), scatter_dimension=0, tiled=True),
        lax.psum_scatter(expert_gain_part, ("fsdp", "ctx"), scatter_dimension=0, tiled=True),
        lax.psum_scatter(query_gain_part, ("fsdp", "ctx"), scatter_dimension=0, tiled=True),
        lax.psum_scatter(key_gain_part, ("fsdp", "ctx"), scatter_dimension=0, tiled=True),
    )
    return (
        hidden_out,
        grad_hidden,
        weight_grads[:, :model_width],
        weight_grads[:, model_width : 2 * model_width],
        weight_grads[:, 2 * model_width : 3 * model_width],
        weight_grads[:, 3 * model_width :],
        gain_grads[0],
        gain_grads[1],
        gain_grads[2],
        gain_grads[3],
        grad_expert_gate,
        grad_expert_up,
        grad_expert_down,
    )


def xor_pairs(size, bit):
    return [(index, index ^ bit) for index in range(size)]


def bits_of(size):
    bit = size // 2
    while bit:
        yield bit
        bit //= 2


def stack_all(value, axis_name):
    size = lax.axis_size(axis_name)
    index = lax.axis_index(axis_name)
    shape = value.shape
    depth = 0
    for bit in bits_of(size):
        other = lax.ppermute(value, axis_name, xor_pairs(size, bit))
        high = (index & bit) != 0
        value = jnp.stack(
            [jnp.where(high, other, value), jnp.where(high, value, other)], axis=depth
        )
        depth += 1
    return value.reshape((size,) + shape)


def sum_all(value, axis_name):
    size = lax.axis_size(axis_name)
    for bit in bits_of(size):
        value = value + lax.ppermute(value, axis_name, xor_pairs(size, bit))
    return value


def sum_scatter(value, axis_name):
    size = lax.axis_size(axis_name)
    index = lax.axis_index(axis_name)
    for bit in bits_of(size):
        half = value.shape[0] // 2
        high = (index & bit) != 0
        lower, upper = value[:half], value[half:]
        other = lax.ppermute(jnp.where(high, lower, upper), axis_name, xor_pairs(size, bit))
        value = jnp.where(high, upper, lower) + other
    return value


def near_blocks(value):
    size = lax.axis_size("fsdp")
    blocks = {0: value}
    for bit in bits_of(size):
        for place in list(blocks):
            blocks[place | bit] = lax.ppermute(blocks[place], "fsdp", xor_pairs(size, bit))
    return [blocks[place] for place in range(size)]


def near_sum(parts, dtype=jnp.bfloat16):
    size = lax.axis_size("fsdp")
    parts = dict(enumerate(parts))
    for bit in reversed(list(bits_of(size))):
        for place in sorted(parts):
            if place & bit:
                other = lax.ppermute(parts[place].astype(dtype), "fsdp", xor_pairs(size, bit))
                near = place ^ bit
                parts[near] = parts[near].astype(jnp.float32) + other.astype(jnp.float32)
        parts = {place: part for place, part in parts.items() if not place & bit}
    return parts[0]


def relative_columns(value):
    size = lax.axis_size("fsdp")
    index = lax.axis_index("fsdp")
    width = value.shape[-1] // size
    return jnp.concatenate(
        [
            lax.dynamic_slice_in_dim(value, (index ^ place) * width, width, axis=-1)
            for place in range(size)
        ],
        axis=-1,
    )


def ring_order(size):
    return list(range(0, size, 2)) + list(range(1, size, 2))[::-1]


def ring_steps(size):
    steps = [0]
    for step in range(1, size // 2):
        steps += [-step, step]
    return steps + [size // 2]


def ring_table(size):
    order = ring_order(size)
    place = {device: spot for spot, device in enumerate(order)}
    return np.array(
        [[order[(place[device] + step) % size] for step in ring_steps(size)] for device in range(size)],
        np.int32,
    )


def ring_pairs(size):
    order = ring_order(size)
    ahead = [(order[spot], order[(spot + 1) % size]) for spot in range(size)]
    return ahead, [(target, source) for source, target in ahead]


def ring_gather(value):
    size = lax.axis_size("ctx")
    ahead, back = ring_pairs(size)
    half = value.shape[1] // 2
    chunks = [value]
    down = up = value
    for _ in range(1, size // 2):
        down = lax.ppermute(down, "ctx", ahead)
        up = lax.ppermute(up, "ctx", back)
        chunks += [down, up]
    chunks.append(
        jnp.concatenate(
            [
                lax.ppermute(down[:, :half], "ctx", ahead),
                lax.ppermute(up[:, half:], "ctx", back),
            ],
            axis=1,
        )
    )
    return chunks


def ring_sum(parts):
    size = lax.axis_size("ctx")
    ahead, back = ring_pairs(size)
    half = parts[0].shape[1] // 2
    by_step = dict(zip(ring_steps(size), parts))
    far = by_step[size // 2]
    down = lax.ppermute(far[:, :half], "ctx", ahead).astype(jnp.float32)
    up = lax.ppermute(far[:, half:], "ctx", back).astype(jnp.float32)
    for step in range(size // 2 - 1, 0, -1):
        toward, from_up = by_step[step].astype(jnp.float32), by_step[-step].astype(jnp.float32)
        if step == size // 2 - 1:
            toward = jnp.concatenate([toward[:, :half] + down, toward[:, half:]], axis=1)
            from_up = jnp.concatenate([from_up[:, :half], from_up[:, half:] + up], axis=1)
        else:
            toward, from_up = toward + down, from_up + up
        down = lax.ppermute(toward.astype(jnp.bfloat16), "ctx", ahead).astype(jnp.float32)
        up = lax.ppermute(from_up.astype(jnp.bfloat16), "ctx", back).astype(jnp.float32)
    return by_step[0].astype(jnp.float32) + down + up


def split_chunks(value, size):
    rows = value.shape[0] // size
    return [value[spot * rows : (spot + 1) * rows] for spot in range(size)]


def per_device_by_heads(
    hidden_in,
    doc_start,
    routes,
    gate_weights,
    w_query,
    w_key,
    w_value,
    w_output,
    gain_attention,
    gain_experts,
    gain_query,
    gain_key,
    expert_gate,
    expert_up,
    expert_down,
    cotangent,
):
    low, wide = jnp.bfloat16, jnp.float32
    tok_rows, model_width = hidden_in.shape
    weight_rows = w_query.shape[0]
    ctx_size = lax.axis_size("ctx")
    fsdp_size = lax.axis_size("fsdp")
    my_ctx = lax.axis_index("ctx")
    my_fsdp = lax.axis_index("fsdp")
    local_experts = expert_gate.shape[0]
    total_experts = local_experts * ctx_size
    heads_here = HEADS // ctx_size
    head_width = heads_here * HD
    stream_len = tok_rows * ctx_size
    order = jnp.asarray(ring_table(ctx_size))[my_ctx]
    place_of = jnp.argmax(order[None, :] == jnp.arange(ctx_size)[:, None], axis=1)
    device_count = ctx_size * fsdp_size
    to_heads = [
        (spot, (spot % fsdp_size) * ctx_size + spot // fsdp_size) for spot in range(device_count)
    ]
    from_heads = [(target, source) for source, target in to_heads]
    everyone = ("fsdp", "ctx")

    hidden = relative_columns(hidden_in)
    scale_one = rms_scale(hidden)
    z_one = hidden * scale_one
    z_chunks = ring_gather(z_one.astype(low))

    gain_rows = gain_attention.astype(wide)[:, None]
    scaled = [(gain_rows * w.astype(wide)).astype(low) for w in (w_query, w_key, w_value)]
    pieces = jnp.concatenate(
        [
            jnp.transpose(w.reshape(weight_rows, ctx_size, head_width), (1, 0, 2))
            for w in scaled
        ],
        axis=2,
    )
    own_columns = lax.all_to_all(pieces, "ctx", split_axis=0, concat_axis=0, tiled=True)
    qkv_matrix = jnp.concatenate(
        near_blocks(own_columns.reshape(ctx_size * weight_rows, 3 * head_width)), axis=0
    )
    output_rows = stack_all(lax.ppermute(w_output, everyone, to_heads), "fsdp")
    output_matrix = relative_columns(output_rows.reshape(head_width, model_width))
    head_gains = stack_all(
        lax.ppermute(jnp.stack([gain_query, gain_key]).astype(wide), everyone, to_heads), "fsdp"
    )
    head_gains = jnp.transpose(head_gains, (1, 0, 2)).reshape(2, head_width)
    query_gain, key_gain = head_gains[0], head_gains[1]
    expert_gain = jnp.concatenate(
        near_blocks(stack_all(gain_experts.astype(wide), "ctx").reshape(-1))
    )

    expert_ids = jnp.arange(total_experts, dtype=routes.dtype)
    own_gates = jnp.sum(
        jnp.where(routes[None] == expert_ids[:, None, None], gate_weights[None], 0.0), axis=-1
    )
    facts = stack_all(
        jnp.concatenate([own_gates, doc_start.astype(wide)[None]], axis=0), "ctx"
    )[order]
    starts = facts[:, total_experts]
    gates = jnp.transpose(
        lax.dynamic_slice_in_dim(facts, my_ctx * local_experts, local_experts, axis=1), (1, 0, 2)
    ).reshape(local_experts, stream_len, 1)
    rows = jnp.arange(tok_rows)
    upto = rows[:, None] <= rows[None, :]
    within = jnp.sum(jnp.where(upto[None], starts[:, :, None], 0.0), axis=1)
    before = order[None, :] < order[:, None]
    segment = within + jnp.sum(jnp.where(before, within[:, -1][None, :], 0.0), axis=1)[:, None]
    place = (order[:, None] * tok_rows + rows[None, :]).astype(wide)
    start_place = jnp.where(starts > 0.5, place, 0.0)
    last = jnp.max(jnp.where(upto[None], start_place[:, :, None], 0.0), axis=1)
    earlier = jnp.max(jnp.where(before, last[:, -1][None, :], 0.0), axis=1)
    position = (place - jnp.maximum(last, earlier[:, None])).reshape(stream_len)
    segment = segment.reshape(stream_len)
    frequency = rope_base ** (-jnp.arange(HD // 2, dtype=wide) * 2.0 / HD)
    angles = position[:, None] * frequency[None, :]
    cosine = jnp.cos(angles)[:, None, :]
    sine_table = jnp.sin(angles)[:, None, :]

    def ctx_mean(sums):
        by_chunk = sums.reshape(sums.shape[0], ctx_size, tok_rows)
        total = sum_all(by_chunk[:, place_of], "ctx")[:, order]
        return total.reshape(sums.shape[0], stream_len, 1) / model_width

    z_rows = jnp.concatenate(z_chunks, axis=0)
    pre = jnp.dot(z_rows, qkv_matrix, preferred_element_type=wide)
    queries_pre = pre[:, :head_width]
    keys_pre = pre[:, head_width : 2 * head_width]
    value_low = pre[:, 2 * head_width :].astype(low).reshape(stream_len, heads_here, HD)
    squares = ctx_mean(
        jnp.stack([jnp.sum(queries_pre * queries_pre, axis=1), jnp.sum(keys_pre * keys_pre, axis=1)])
    )
    query_scale = lax.rsqrt(squares[0] + epsilon)
    key_scale = lax.rsqrt(squares[1] + epsilon)
    z_query = queries_pre * query_scale
    z_key = keys_pre * key_scale
    query_rot = (
        rotate((z_query * query_gain).reshape(stream_len, heads_here, HD), cosine, sine_table)
        * HD ** (-0.5)
    ).astype(low)
    key_rot = rotate(
        (z_key * key_gain).reshape(stream_len, heads_here, HD), cosine, sine_table
    ).astype(low)
    allowed = (segment[:, None] == segment[None, :])[None]
    scores = jnp.einsum("qhd,khd->hqk", query_rot, key_rot, preferred_element_type=wide)
    scores = jnp.where(allowed, scores, masked_score)
    weights = jnp.exp(scores - jnp.max(scores, axis=-1, keepdims=True))
    probs = weights / jnp.sum(weights, axis=-1, keepdims=True)
    probs_low = probs.astype(low)
    attended = jnp.einsum("hqk,khd->qhd", probs_low, value_low, preferred_element_type=wide)
    attended_low = attended.astype(low).reshape(stream_len, head_width)
    projected = jnp.dot(attended_low, output_matrix, preferred_element_type=wide).astype(low)
    mixed = hidden + ring_sum(split_chunks(projected, ctx_size))

    scale_two = rms_scale(mixed)
    z_two = mixed * scale_two
    x_rows = jnp.concatenate(ring_gather((z_two * expert_gain).astype(low)), axis=0)
    cotangent_own = relative_columns(cotangent)
    cot_rows = jnp.concatenate(ring_gather(cotangent_own.astype(low)), axis=0)
    gate_full = jnp.concatenate(near_blocks(expert_gate), axis=1)
    up_full = jnp.concatenate(near_blocks(expert_up), axis=1)
    down_full = jnp.concatenate(near_blocks(expert_down), axis=2)
    gate_pre = jnp.einsum("td,jdf->jtf", x_rows, gate_full, preferred_element_type=wide)
    up_pre = jnp.einsum("td,jdf->jtf", x_rows, up_full, preferred_element_type=wide)
    sigmoid_gate = jax.nn.sigmoid(gate_pre)
    silu_gate = gate_pre * sigmoid_gate
    activated = (silu_gate * up_pre * gates).astype(low)
    grad_act = gates * jnp.einsum("td,jfd->jtf", cot_rows, down_full, preferred_element_type=wide)
    grad_gate = (grad_act * up_pre * sigmoid_gate * (1.0 + gate_pre * (1.0 - sigmoid_gate))).astype(
        low
    )
    grad_up = (grad_act * silu_gate).astype(low)
    grad_x = (
        jnp.einsum("jtf,jdf->td", grad_gate, gate_full, preferred_element_type=wide)
        + jnp.einsum("jtf,jdf->td", grad_up, up_full, preferred_element_type=wide)
    ).astype(low)
    grad_normed_two = ring_sum(split_chunks(grad_x, ctx_size))
    produced = jnp.einsum("jtf,jfd->td", activated, down_full, preferred_element_type=wide)
    hidden_out = mixed + ring_sum(split_chunks(produced.astype(low), ctx_size))

    block_width = model_width // fsdp_size

    def column_blocks(value):
        return [
            value[:, spot * block_width : (spot + 1) * block_width] for spot in range(fsdp_size)
        ]

    x_blocks, cot_blocks = column_blocks(x_rows), column_blocks(cot_rows)
    grad_expert_down = near_sum(
        [
            jnp.einsum("jtf,td->jfd", activated, block, preferred_element_type=wide).astype(low)
            for block in cot_blocks
        ]
    )
    grad_expert_gate = near_sum(
        [
            jnp.einsum("td,jtf->jdf", block, grad_gate, preferred_element_type=wide).astype(low)
            for block in x_blocks
        ]
    )
    grad_expert_up = near_sum(
        [
            jnp.einsum("td,jtf->jdf", block, grad_up, preferred_element_type=wide).astype(low)
            for block in x_blocks
        ]
    )

    weighted_two = grad_normed_two * expert_gain
    grad_mixed = cotangent_own + scale_two * (
        weighted_two - z_two * jnp.mean(z_two * weighted_two, axis=-1, keepdims=True)
    )
    expert_gain_part = jnp.sum(grad_normed_two * z_two, axis=0)
    grad_gain_experts = sum_scatter(near_sum(jnp.split(expert_gain_part, fsdp_size), wide), "ctx")
    grad_attn = jnp.concatenate(ring_gather(grad_mixed.astype(low)), axis=0)

    grad_heads = (
        times_transpose(grad_attn, output_matrix).astype(low).reshape(stream_len, heads_here, HD)
    )
    row_dots = jnp.transpose(jnp.sum(grad_heads.astype(wide) * attended, axis=-1))[..., None]
    grad_probs = jnp.einsum("qhd,khd->hqk", grad_heads, value_low, preferred_element_type=wide)
    grad_scores = (probs * (grad_probs - row_dots)).astype(low)
    grad_query_rot = jnp.einsum("hqk,khd->qhd", grad_scores, key_rot, preferred_element_type=wide)
    grad_key_rot = jnp.einsum("hqk,qhd->khd", grad_scores, query_rot, preferred_element_type=wide)
    grad_value = jnp.einsum("hqk,qhd->khd", probs_low, grad_heads, preferred_element_type=wide)
    grad_query_normed = (
        rotate_back(grad_query_rot, cosine, sine_table) * HD ** (-0.5)
    ).reshape(stream_len, head_width)
    grad_key_normed = rotate_back(grad_key_rot, cosine, sine_table).reshape(stream_len, head_width)
    weighted_query = grad_query_normed * query_gain
    weighted_key = grad_key_normed * key_gain
    means = ctx_mean(
        jnp.stack([jnp.sum(z_query * weighted_query, axis=1), jnp.sum(z_key * weighted_key, axis=1)])
    )
    grads_pre = jnp.concatenate(
        [
            (query_scale * (weighted_query - z_query * means[0])).astype(low),
            (key_scale * (weighted_key - z_key * means[1])).astype(low),
            grad_value.reshape(stream_len, head_width).astype(low),
        ],
        axis=1,
    )
    weighted_one = ring_sum(
        split_chunks(times_transpose(grads_pre, qkv_matrix).astype(low), ctx_size)
    )
    grad_hidden = grad_mixed + scale_one * (
        weighted_one - z_one * jnp.mean(z_one * weighted_one, axis=-1, keepdims=True)
    )

    def over_rows(left, right):
        return lax.dot_general(left, right, (((0,), (0,)), ((), ())), preferred_element_type=wide)

    qkv_part = over_rows(z_rows, grads_pre).astype(low)
    qkv_sum = near_sum([qkv_part[spot * block_width :][:block_width] for spot in range(fsdp_size)])
    qkv_sum = lax.all_to_all(
        qkv_sum.reshape(ctx_size, weight_rows, 3 * head_width),
        "ctx",
        split_axis=0,
        concat_axis=0,
        tiled=True,
    )
    unscaled = [
        jnp.transpose(
            qkv_sum[:, :, spot * head_width : (spot + 1) * head_width], (1, 0, 2)
        ).reshape(weight_rows, model_width)
        for spot in range(3)
    ]
    grad_gain_attention = sum(
        jnp.sum(w.astype(wide) * part, axis=1) for w, part in zip((w_query, w_key, w_value), unscaled)
    )

    def to_owner(part):
        blocks = part.reshape((fsdp_size, weight_rows) + part.shape[1:])
        return [
            lax.dynamic_index_in_dim(blocks, my_fsdp ^ spot, axis=0, keepdims=False)
            for spot in range(fsdp_size)
        ]

    output_part = relative_columns(over_rows(attended_low, grad_attn)).astype(low)
    grad_w_output = lax.ppermute(near_sum(to_owner(output_part)), everyone, from_heads)
    gain_part = jnp.stack(
        [jnp.sum(grad_query_normed * z_query, axis=0), jnp.sum(grad_key_normed * z_key, axis=0)],
        axis=1,
    )
    head_gain_grads = lax.ppermute(near_sum(to_owner(gain_part), wide), everyone, from_heads)
    return (
        relative_columns(hidden_out),
        relative_columns(grad_hidden),
        gain_rows * unscaled[0],
        gain_rows * unscaled[1],
        gain_rows * unscaled[2],
        grad_w_output,
        grad_gain_attention,
        grad_gain_experts,
        head_gain_grads[:, 0],
        head_gain_grads[:, 1],
        grad_expert_gate,
        grad_expert_up,
        grad_expert_down,
    )


def solution(mesh):
    placed = (
        P(("fsdp", "ctx"), None),
        P(("fsdp", "ctx")),
        P(("fsdp", "ctx"), None),
        P(("fsdp", "ctx"), None),
        P(("fsdp", "ctx"), None),
        P(("fsdp", "ctx"), None),
        P(("fsdp", "ctx"), None),
        P(("fsdp", "ctx"), None),
        P(("fsdp", "ctx")),
        P(("fsdp", "ctx")),
        P(("fsdp", "ctx")),
        P(("fsdp", "ctx")),
        P("ctx", "fsdp", None),
        P("ctx", "fsdp", None),
        P("ctx", None, "fsdp"),
        P(("fsdp", "ctx"), None),
    )
    ctx_size = mesh.shape["ctx"]
    body = per_device_by_heads if HEADS % ctx_size == 0 else per_device
    return jax.shard_map(
        body,
        mesh=mesh,
        in_specs=placed,
        out_specs=(
            P(("fsdp", "ctx"), None),
            P(("fsdp", "ctx"), None),
            P(("fsdp", "ctx"), None),
            P(("fsdp", "ctx"), None),
            P(("fsdp", "ctx"), None),
            P(("fsdp", "ctx"), None),
            P(("fsdp", "ctx")),
            P(("fsdp", "ctx")),
            P(("fsdp", "ctx")),
            P(("fsdp", "ctx")),
            P("ctx", "fsdp", None),
            P("ctx", "fsdp", None),
            P("ctx", None, "fsdp"),
        ),
        check_vma=False,
    )
```
